128 devices in a mesh: dp: 8 (over y_hi, z), ctx: 16 (over y_lo, x, core).
Axes of the slice: x: 4, y: 4 (y_hi: 2, y_lo: 2; y = y_hi * 2 + y_lo), z: 4, core: 2. Of those that a mesh axis runs over, the one named last changes fastest.
Arguments:
- hidden: bfloat16 [8, 4096, 8192], P('dp', 'ctx'), may hold values from -6 to 6
- queries: bfloat16 [8, 4096, 4096], P('dp', 'ctx')
- layout: int32 [8, 32], P('dp'), may hold values from 0 to 31, each once within a row
- boundary: int32 [8], P('dp'), may hold values from 1 to 4095
- key_matrix: bfloat16 [8192, 512], P(('dp', 'ctx')), may hold values from -0.0625 to 0.0625
- value_matrix: bfloat16 [8192, 512], P(('dp', 'ctx')), may hold values from -0.0625 to 0.0625
Outputs:
- attended: bfloat16 [8, 4096, 4096], P('dp', 'ctx')
The draws below stay inside these ranges and needn't reach their ends.
Inputs may be any that keep to these rules, and one draw needn't show every extreme that they name: Each row holds every block number of 0 to 31 once; local block b of ctx index c is layout[2 c + b].
All inputs are finite; a program needn't handle non-finite values.
Results may differ from the reference program's by a relative error of at most 0.011.
Values may be sent and summed in bfloat16 or wider, within the bound.
A program may use at most 320 MiB of HBM per device.

```python
import jax
import jax.numpy as jnp
from jax import lax

MODEL_WIDTH = 8192
HQ = 32
KEY_VALUE_HEADS = 4
HEAD_WIDTH = 128
TOKENS_PER_SHARD = 256
QUERY_PER_KV = 8
HALF = 128
NBLK = 32
WINDOW_TOKENS = 4096
WINDOWS = 8


def draw_queries(key, part):
    first = jax.random.fold_in(key, 0)
    base = jnp.clip(jax.random.normal(first, (WINDOWS, WINDOW_TOKENS, HQ * HEAD_WIDTH), jnp.float32), -6.0, 6.0) * 2.5
    return base.astype(jnp.bfloat16)


def set_ends(entries, own_key, low, high):
    index_at = [jax.random.randint(jax.random.fold_in(own_key, axis), (), 0, length) for axis, length in enumerate(entries.shape)]
    widest = entries.shape.index(max(entries.shape))
    beside = index_at[:widest] + [(index_at[widest] + 1) % entries.shape[widest]] + index_at[widest + 1:]
    return entries.at[tuple(index_at)].set(low).at[tuple(beside)].set(high)


def block_scale(own_key, dims, shards, smallest, top_value):
    gain, own = 1.0, jax.random.fold_in(own_key, 6)
    for position, shards_of in shards:
        draws = jnp.exp(jax.random.uniform(jax.random.fold_in(own, position), (shards_of,), jnp.float32, smallest / len(shards), top_value / len(shards)))
        gain = gain * jnp.repeat(draws, dims[position] // shards_of).reshape([-1 if axis == position else 1 for axis in range(len(dims))])
    return gain


def centred(rng, dims, scale, most, cuts=(), held_as=jnp.bfloat16):
    values = jax.random.normal(rng, dims, jnp.float32) * scale
    if len(cuts) > 0:
        values = block_scale(rng, dims, cuts, -0.22, 0.18) * values
    return jnp.clip(values, min=-most, max=most).astype(held_as)


def setup_inputs(seed: int = 0) -> dict:
    arg_keys = jax.random.split(jax.random.key(seed), 7)
    return {
        "hidden": centred(arg_keys[0], (WINDOWS, WINDOW_TOKENS, MODEL_WIDTH), 1.0, 6.0, ((0, 8), (1, 16))),
        "queries": draw_queries(jax.random.fold_in(arg_keys[6], 71), 0),
        "layout": jax.vmap(lambda own: jax.random.permutation(own, NBLK))(jax.random.split(arg_keys[2], WINDOWS)).reshape((WINDOWS, NBLK)).astype(jnp.int32),
        "boundary": set_ends(jax.random.randint(arg_keys[3], (WINDOWS,), 1, WINDOW_TOKENS), jax.random.fold_in(arg_keys[3], 1), 1, WINDOW_TOKENS - 1).astype(jnp.int32),
        "key_matrix": centred(arg_keys[4], (MODEL_WIDTH, KEY_VALUE_HEADS * HEAD_WIDTH), MODEL_WIDTH ** -0.5, 0.0625, ((0, 128),)),
        "value_matrix": centred(arg_keys[5], (MODEL_WIDTH, KEY_VALUE_HEADS * HEAD_WIDTH), MODEL_WIDTH ** -0.5, 0.0625, ((0, 128),)),
    }


def reference(hidden, queries, layout, boundary, key_matrix, value_matrix):
    scale = HEAD_WIDTH ** -0.5

    def window(items):
        tokens, requested, order, start = items
        key_tensor = jnp.dot(tokens, key_matrix, preferred_element_type=jnp.float32).astype(jnp.bfloat16)
        value_tensor = jnp.dot(tokens, value_matrix, preferred_element_type=jnp.float32).astype(jnp.bfloat16)
        index = jnp.arange(WINDOW_TOKENS, dtype=jnp.int32)
        where_at = (order[index // HALF] * HALF + index % HALF).astype(jnp.int32)
        key_row_set = key_tensor.reshape(WINDOW_TOKENS, KEY_VALUE_HEADS, HEAD_WIDTH).astype(jnp.float32)
        value_row_set = value_tensor.reshape(WINDOW_TOKENS, KEY_VALUE_HEADS, HEAD_WIDTH).astype(jnp.float32)
        block_list = requested.reshape(WINDOW_TOKENS // TOKENS_PER_SHARD, TOKENS_PER_SHARD, KEY_VALUE_HEADS, QUERY_PER_KV, HEAD_WIDTH)
        block_pos = where_at.reshape(WINDOW_TOKENS // TOKENS_PER_SHARD, TOKENS_PER_SHARD)

        def block(parts):
            query_rows, query_pos = parts
            scores = jnp.einsum("qgha,kga->ghqk", query_rows.astype(jnp.float32), key_row_set) * scale
            allowed = (where_at[None, :] <= query_pos[:, None]) & ((where_at[None, :] >= start) | (query_pos[:, None] < start))
            scores = jnp.where(allowed, scores, -1e30)
            peak = jnp.max(scores, axis=-1)
            weights = jnp.where(allowed, jnp.exp(scores - peak[..., None]), 0.0)
            total = jnp.sum(weights, axis=-1)
            probs = lax.optimization_barrier(weights.astype(jnp.bfloat16))
            summed = jnp.einsum("ghqk,kga->ghqa", probs.astype(jnp.float32), value_row_set)
            result = summed / total[..., None]
            return result.transpose(2, 0, 1, 3).reshape(TOKENS_PER_SHARD, HQ * HEAD_WIDTH).astype(jnp.bfloat16)

        return lax.map(block, (block_list, block_pos)).reshape(WINDOW_TOKENS, HQ * HEAD_WIDTH)

    return lax.map(window, (hidden, queries, layout, boundary))
```

```python
import functools

import jax
import jax.numpy as jnp
from jax import lax
from jax.experimental import pallas as pl
from jax.experimental.pallas import tpu as pltpu
from jax.sharding import PartitionSpec as P

HEAD_WIDTH = 128
KEY_TILE = 512
NEG = -1e30


def attend_kernel(flag_ref, bound_ref, q_ref, k_ref, v_ref, qp_ref, kp_ref, o_ref, m_sc, l_sc, acc_sc):
    step = pl.program_id(0)
    group_size = m_sc.shape[0]
    scale = HEAD_WIDTH ** (-0.5)

    @pl.when(step == 0)
    def _():
        m_sc[...] = jnp.full_like(m_sc, NEG)
        l_sc[...] = jnp.zeros_like(l_sc)
        acc_sc[...] = jnp.zeros_like(acc_sc)

    def update(masked):
        k = k_ref[...]
        v = v_ref[...]
        if masked:
            start = bound_ref[0]
            qp = qp_ref[...]
            kp = kp_ref[...]
            allowed = (kp <= qp) & ((kp >= start) | (qp < start))
        for j in range(group_size):
            q = q_ref[:, j * HEAD_WIDTH:(j + 1) * HEAD_WIDTH]
            s = lax.dot_general(q, k, (((1,), (1,)), ((), ())), preferred_element_type=jnp.float32) * scale
            if masked:
                s = jnp.where(allowed, s, NEG)
            m_prev = m_sc[j]
            m_new = jnp.maximum(m_prev, jnp.max(s, axis=1, keepdims=True))
            alpha = jnp.exp(m_prev - m_new)
            p = jnp.exp(s - m_new)
            l_sc[j] = alpha * l_sc[j] + jnp.sum(p, axis=1, keepdims=True)
            acc_sc[j] = alpha * acc_sc[j] + jnp.dot(
                p.astype(jnp.bfloat16), v, preferred_element_type=jnp.float32
            )
            m_sc[j] = m_new

    flag = flag_ref[step]

    @pl.when(flag == 1)
    def _():
        update(True)

    @pl.when(flag == 2)
    def _():
        update(False)

    @pl.when(step == pl.num_programs(0) - 1)
    def _():
        for j in range(group_size):
            o_ref[:, j * HEAD_WIDTH:(j + 1) * HEAD_WIDTH] = (acc_sc[j] / l_sc[j]).astype(o_ref.dtype)


def attend_group(flags, bound, queries, kv, qpos, kpos, group_size):
    rows = queries.shape[0]
    keys = kv.shape[0]
    tiles = keys // KEY_TILE
    width = group_size * HEAD_WIDTH
    flops = 4 * rows * keys * width
    return pl.pallas_call(
        functools.partial(attend_kernel),
        out_shape=jax.ShapeDtypeStruct((rows, width), jnp.bfloat16),
        grid_spec=pltpu.PrefetchScalarGridSpec(
            num_scalar_prefetch=2,
            grid=(tiles,),
            in_specs=[
                pl.BlockSpec((rows, width), lambda i, f, b: (0, 0)),
                pl.BlockSpec((KEY_TILE, HEAD_WIDTH), lambda i, f, b: (i, 0)),
                pl.BlockSpec((KEY_TILE, HEAD_WIDTH), lambda i, f, b: (i, 1)),
                pl.BlockSpec((rows, 1), lambda i, f, b: (0, 0)),
                pl.BlockSpec((1, KEY_TILE), lambda i, f, b: (0, i)),
            ],
            out_specs=pl.BlockSpec((rows, width), lambda i, f, b: (0, 0)),
            scratch_shapes=[
                pltpu.VMEM((group_size, rows, 1), jnp.float32),
                pltpu.VMEM((group_size, rows, 1), jnp.float32),
                pltpu.VMEM((group_size, rows, HEAD_WIDTH), jnp.float32),
            ],
        ),
        compiler_params=pltpu.CompilerParams(dimension_semantics=("arbitrary",)),
        cost_estimate=pl.CostEstimate(
            flops=flops,
            transcendentals=rows * keys * group_size,
            bytes_accessed=2 * (rows * width * 2 + keys * 2 * HEAD_WIDTH),
        ),
    )(flags, bound, queries, kv, kv, qpos, kpos)


def per_device(hidden, queries, layout, boundary, key_matrix, value_matrix):
    rows = hidden.shape[1]
    kv_width = key_matrix.shape[1]
    kv_heads = kv_width // HEAD_WIDTH
    group_size = queries.shape[2] // kv_width
    block = rows // 2
    ctx_count = lax.axis_size("ctx")
    dp_count = lax.axis_size("dp")
    here = lax.axis_index("ctx")
    tokens = hidden[0]
    order = layout[0]
    start_doc = boundary[0]
    window = rows * ctx_count

    kpos = (order[:, None] * block + jnp.arange(block, dtype=jnp.int32)[None, :]).reshape(window)
    qpos = lax.dynamic_slice(kpos, (here * rows,), (rows,))
    allowed = (kpos[None, :] <= qpos[:, None]) & ((kpos[None, :] >= start_doc) | (qpos[:, None] < start_doc))
    tiles = allowed.reshape(rows, window // KEY_TILE, KEY_TILE)
    some = jnp.any(tiles, axis=(0, 2))
    every = jnp.all(tiles, axis=(0, 2))
    flags = jnp.where(every, 2, jnp.where(some, 1, 0)).astype(jnp.int32)
    bound = boundary.astype(jnp.int32)
    qpos2 = qpos[:, None]
    kpos2 = kpos[None, :]

    feat = key_matrix.shape[0]
    outs = []
    for g in range(kv_heads):
        cols = slice(g * HEAD_WIDTH, (g + 1) * HEAD_WIDTH)
        w = jnp.concatenate((key_matrix[:, cols], value_matrix[:, cols]), axis=1)
        w = lax.all_gather(w, "dp", axis=0, tiled=True)
        w = lax.all_gather(w, "ctx", axis=0, tiled=True)
        w = w.reshape(ctx_count, dp_count, feat, 2 * HEAD_WIDTH)
        part = jnp.einsum(
            "tdcr,cdrn->tn",
            tokens.reshape(rows, dp_count, ctx_count, feat),
            w,
            preferred_element_type=jnp.float32,
        ).astype(jnp.bfloat16)
        kv = lax.all_gather(part, "ctx", axis=0, tiled=True)
        q_g = queries[0][:, g * group_size * HEAD_WIDTH:(g + 1) * group_size * HEAD_WIDTH]
        outs.append(attend_group(flags, bound, q_g, kv, qpos2, kpos2, group_size))
    return jnp.concatenate(outs, axis=1)[None]


def solution(mesh):
    in_specs = (
        P("dp", "ctx", None),
        P("dp", "ctx", None),
        P("dp", None),
        P("dp"),
        P(("dp", "ctx"), None),
        P(("dp", "ctx"), None),
    )
    out_specs = P("dp", "ctx", None)
    return jax.shard_map(
        per_device, mesh=mesh, in_specs=in_specs, out_specs=out_specs, check_vma=False
    )
```
